32 devices in a mesh: space: 8 (over y, x, core), tm: 4 (over z).
Axes of the slice: x: 2, y: 2, z: 4, core: 2. Of those that a mesh axis runs over, the one named last changes fastest.
Arguments:
- series: bfloat16 [16384, 2, 512], P('space', None, 'tm'), may hold values from -6 to 6
- space_basis: bfloat16 [16384, 16384], P('space', 'tm'), may hold values from -0.046875 to 0.046875
- time_basis: bfloat16 [512, 512], P('tm'), may hold values from -0.25 to 0.25
- space_eig: float32 [16384], replicated, may hold values from 0.3 to 3
- time_eig: float32 [512], replicated, may hold values from 0.3 to 3
Outputs:
- alpha: bfloat16 [16384, 2, 512], P('space', None, 'tm')
- grad_space: bfloat16 [16384, 8, 2048], P('space', None, 'tm')
The draws below stay inside these ranges and needn't reach their ends.
All inputs are finite; a program needn't handle non-finite values.
Results may differ from the reference program's by a relative error of at most 0.0063.
Values may be sent and summed in bfloat16 or wider, within the bound.
A program may use at most 128 MiB of HBM per device.

```python
import math
import jax
import jax.numpy as jnp

STATIONS = 16384
TIMES = 512
REPS = 2
N_SPACE = 8


def steps_of(stream_key, shape, cuts, smallest, high):
    level, own = 1.0, jax.random.fold_in(stream_key, 6)
    for dim, blocks in cuts:
        heights = jnp.exp(jax.random.uniform(jax.random.fold_in(own, dim), (blocks,), jnp.float32, smallest / len(cuts), high / len(cuts)))
        level = level * jnp.repeat(heights, shape[dim] // blocks).reshape([-1 if axis == dim else 1 for axis in range(len(shape))])
    return level


def bell_draw(stream_key, extent, spread, reach, split=(), held_as=jnp.bfloat16):
    entries = jax.random.normal(stream_key, extent, jnp.float32) * spread
    if len(split) > 0:
        entries = steps_of(stream_key, extent, split, -0.22, 0.18) * entries
    return jnp.clip(entries, min=-reach, max=reach).astype(held_as)


def setup_inputs(seed: int = 0) -> dict:
    splits = jax.random.split(jax.random.key(seed), 6)
    return {
        "series": bell_draw(splits[0], (STATIONS, REPS, TIMES), 1.0, 6.0, ((0, 8), (2, 4))),
        "space_basis": bell_draw(splits[1], (STATIONS, STATIONS), STATIONS ** -0.5, 0.046875, ((0, 8), (1, 4))),
        "time_basis": bell_draw(splits[2], (TIMES, TIMES), TIMES ** -0.5, 0.25, ((0, 4),)),
        "space_eig": jnp.clip(jnp.exp(jax.random.uniform(splits[3], (STATIONS,), jnp.float32, math.log(0.3), math.log(3.0))), 0.3, 3.0),
        "time_eig": jnp.clip(jnp.exp(jax.random.uniform(splits[4], (TIMES,), jnp.float32, math.log(0.3), math.log(3.0))), 0.3, 3.0),
    }


def reference(series, space_basis, time_basis, space_eig, time_eig):
    flat = series.reshape(STATIONS * REPS, TIMES)
    rotated = jnp.dot(flat, time_basis, preferred_element_type=jnp.float32).astype(jnp.bfloat16)
    rotated = rotated.reshape(STATIONS, REPS * TIMES)
    spectral = jnp.dot(space_basis.T, rotated, preferred_element_type=jnp.float32)
    denom = space_eig[:, None, None] * time_eig[None, None, :] + 0.1
    scaled_spec = (spectral.reshape(STATIONS, REPS, TIMES) / denom).astype(jnp.bfloat16)
    scaled_spec = scaled_spec.reshape(STATIONS, REPS * TIMES)
    back = jnp.dot(space_basis, scaled_spec, preferred_element_type=jnp.float32).astype(jnp.bfloat16)
    alpha = jnp.dot(back.reshape(STATIONS * REPS, TIMES), time_basis.T, preferred_element_type=jnp.float32)
    alpha = alpha.astype(jnp.bfloat16).reshape(STATIONS, REPS, TIMES)
    weighted = back.reshape(STATIONS, REPS, TIMES).astype(jnp.float32) * time_eig[None, None, :]
    weighted = (weighted / (REPS * TIMES)).astype(jnp.bfloat16).reshape(STATIONS, REPS * TIMES)
    grad = jnp.dot(weighted, back.T, preferred_element_type=jnp.float32).astype(jnp.bfloat16)
    return alpha, grad.reshape(STATIONS, N_SPACE, STATIONS // N_SPACE)
```

```python
import jax
import jax.numpy as jnp
from jax import lax
from jax.sharding import PartitionSpec as P


F32 = jnp.float32
BF16 = jnp.bfloat16


def flip(x, axis, bit):
    n = lax.axis_size(axis)
    return lax.ppermute(x, axis, [(i, i ^ bit) for i in range(n)])


def pick(x, index, axis):
    return lax.dynamic_index_in_dim(x, index, axis, keepdims=False)


def line_gather(x, axis):
    n = lax.axis_size(axis)
    up, down, from_below, from_above = x, x, [], []
    for k in range(1, n):
        up = lax.ppermute(up, axis, [(i, i + 1) for i in range(k - 1, n - 1)])
        down = lax.ppermute(down, axis, [(i, i - 1) for i in range(1, n - k + 1)])
        from_below.append(up)
        from_above.append(down)
    return from_below, from_above


def line_reduce_scatter(blocks, axis):
    n = lax.axis_size(axis)
    me = lax.axis_index(axis)
    up = down = None
    for t in range(n - 1):
        send_up = pick(blocks, jnp.minimum(me + n - 1 - t, n - 1), 0)
        send_down = pick(blocks, jnp.maximum(me - (n - 1 - t), 0), 0)
        if t > 0:
            send_up = send_up + up.astype(F32)
            send_down = send_down + down.astype(F32)
        up = lax.ppermute(send_up.astype(BF16), axis, [(i, i + 1) for i in range(t + 1)])
        down = lax.ppermute(
            send_down.astype(BF16), axis, [(i, i - 1) for i in range(n - 1 - t, n)]
        )
    return pick(blocks, me, 0) + (up.astype(F32) + down.astype(F32))


def line_assemble(own, from_below, from_above, axis):
    n = lax.axis_size(axis)
    me = lax.axis_index(axis)
    whole = jnp.zeros((n,) + own.shape, own.dtype)
    whole = lax.dynamic_update_index_in_dim(whole, own, me, 0)
    for k in range(1, n):
        piece = jnp.where(me >= k, from_below[k - 1], from_above[n - k - 1])
        whole = lax.dynamic_update_index_in_dim(whole, piece, lax.rem(me - k + n, n), 0)
    return whole.reshape((-1,) + own.shape[1:])


def halves(axis):
    n = lax.axis_size(axis)
    me = lax.axis_index(axis)
    bits = []
    size = n // 2
    while size >= 1:
        bits.append((size, lax.rem(me // size, 2)))
        size //= 2
    return bits


def stage_orders(count):
    outer = list(range(count - 1))
    return [outer, outer[::-1]] if count > 2 else [outer]


def space_reduce_scatter(x, axis):
    bits = halves(axis)
    count = len(bits)
    rows, cols = x.shape
    own = rows // 2**count
    x = x.reshape((2,) * count + (own, cols))
    flip_size, bit = bits[-1]
    sent = flip(pick(x, 1 - bit, count - 1), axis, flip_size)
    x = pick(x, bit, count - 1) + sent
    orders = stage_orders(count)
    part = own // len(orders)
    done = []
    for p, order in enumerate(orders):
        y = lax.slice_in_dim(x, p * part, (p + 1) * part, axis=count - 1)
        left = list(range(count - 1))
        for b in order:
            at = left.index(b)
            flip_size, bit = bits[b]
            got = flip(pick(y, 1 - bit, at).astype(BF16), axis, flip_size)
            y = pick(y, bit, at) + got.astype(F32)
            left.remove(b)
        done.append(y)
    return jnp.concatenate(done, axis=0) if len(done) > 1 else done[0]


def join(own, got, bit, at):
    return jnp.where(bit == 0, jnp.stack([own, got], at), jnp.stack([got, own], at))


def space_all_gather(x, axis):
    bits = halves(axis)
    count = len(bits)
    own, cols = x.shape
    orders = stage_orders(count)
    part = own // len(orders)
    done = []
    for p, order in enumerate(orders):
        y = lax.slice_in_dim(x, p * part, (p + 1) * part, axis=0)
        have = []
        for b in order[::-1]:
            have = sorted(have + [b])
            flip_size, bit = bits[b]
            y = join(y, flip(y, axis, flip_size), bit, have.index(b))
        done.append(y)
    y = jnp.concatenate(done, axis=count - 1) if len(done) > 1 else done[0]
    flip_size, bit = bits[-1]
    y = join(y, flip(y, axis, flip_size), bit, count - 1)
    return y.reshape(own * 2**count, cols)


def per_device(series, space_basis, time_basis, space_eig, time_eig):
    space_count = lax.axis_size("space")
    time_count = lax.axis_size("tm")
    space_idx = lax.axis_index("space")
    time_idx = lax.axis_index("tm")
    row_count, reps, _ = series.shape
    times = time_basis.shape[1]
    col_block = space_basis.shape[1]
    sub_rows = row_count // time_count
    own_cols = col_block // space_count
    eig_rows = lax.dynamic_slice_in_dim(
        space_eig, time_idx * col_block + space_idx * own_cols, own_cols
    )
    denom = eig_rows[:, None] * time_eig[None, :] + 0.1
    contract_rows = (((0,), (0,)), ((), ()))
    contract_last = (((1,), (1,)), ((), ()))

    basis_below, basis_above = line_gather(time_basis, "tm")
    alphas, grad = [], None
    for q in range(reps):
        mine = series[:, q, :]
        below, above = line_gather(mine, "tm")
        rotated = jnp.dot(mine, time_basis, preferred_element_type=F32)
        for k in range(time_count - 1):
            rotated = rotated + jnp.dot(
                jnp.concatenate([below[k], above[k]], 1),
                jnp.concatenate([basis_below[k], basis_above[k]], 0),
                preferred_element_type=F32,
            )
        rotated = rotated.astype(BF16)
        partial = lax.dot_general(
            space_basis, rotated, contract_rows, preferred_element_type=F32
        )
        spectral = space_reduce_scatter(partial, "space")
        scaled = space_all_gather((spectral / denom).astype(BF16), "space")
        back_part = jnp.dot(space_basis, scaled, preferred_element_type=F32)
        back_sub = line_reduce_scatter(
            back_part.reshape(time_count, sub_rows, times), "tm"
        ).astype(BF16)
        columns = space_all_gather(back_sub, "space")
        rows = line_assemble(back_sub, *line_gather(back_sub, "tm"), "tm")
        alpha = lax.dot_general(rows, time_basis, contract_last, preferred_element_type=F32)
        alphas.append(alpha.astype(BF16))
        weighted = (rows.astype(F32) * time_eig[None, :] / (reps * times)).astype(BF16)
        part = lax.dot_general(weighted, columns, contract_last, preferred_element_type=F32)
        grad = part if grad is None else grad + part
    grad = grad.astype(BF16).reshape(row_count, space_count, sub_rows)
    return (jnp.stack(alphas, 1), grad)


def solution(mesh):
    return jax.shard_map(
        per_device,
        mesh=mesh,
        in_specs=(P("space", None, "tm"), P("space", "tm"), P("tm", None), P(), P()),
        out_specs=(P("space", None, "tm"), P("space", None, "tm")),
        check_vma=False,
    )
```

```python
import jax
import jax.numpy as jnp
from jax import lax
from jax.experimental import pallas as pl
from jax.experimental.pallas import tpu as pltpu
from jax.sharding import PartitionSpec as P


F32 = jnp.float32
BF16 = jnp.bfloat16


def flip(x, axis, bit):
    n = lax.axis_size(axis)
    return lax.ppermute(x, axis, [(i, i ^ bit) for i in range(n)])


def pick(x, index, axis):
    return lax.dynamic_index_in_dim(x, index, axis, keepdims=False)


def line_gather(x, axis):
    n = lax.axis_size(axis)
    up, down, from_below, from_above = x, x, [], []
    for k in range(1, n):
        up = lax.ppermute(up, axis, [(i, i + 1) for i in range(k - 1, n - 1)])
        down = lax.ppermute(down, axis, [(i, i - 1) for i in range(1, n - k + 1)])
        from_below.append(up)
        from_above.append(down)
    return from_below, from_above


def line_reduce_scatter(blocks, axis):
    n = lax.axis_size(axis)
    me = lax.axis_index(axis)
    up = down = None
    for t in range(n - 1):
        send_up = pick(blocks, jnp.minimum(me + n - 1 - t, n - 1), 0)
        send_down = pick(blocks, jnp.maximum(me - (n - 1 - t), 0), 0)
        if t > 0:
            send_up = send_up + up.astype(F32)
            send_down = send_down + down.astype(F32)
        up = lax.ppermute(send_up.astype(BF16), axis, [(i, i + 1) for i in range(t + 1)])
        down = lax.ppermute(
            send_down.astype(BF16), axis, [(i, i - 1) for i in range(n - 1 - t, n)]
        )
    return pick(blocks, me, 0) + (up.astype(F32) + down.astype(F32))


def line_assemble(own, from_below, from_above, axis):
    n = lax.axis_size(axis)
    me = lax.axis_index(axis)
    whole = jnp.zeros((n,) + own.shape, own.dtype)
    whole = lax.dynamic_update_index_in_dim(whole, own, me, 0)
    for k in range(1, n):
        piece = jnp.where(me >= k, from_below[k - 1], from_above[n - k - 1])
        whole = lax.dynamic_update_index_in_dim(whole, piece, lax.rem(me - k + n, n), 0)
    return whole.reshape((-1,) + own.shape[1:])


def halves(axis):
    n = lax.axis_size(axis)
    me = lax.axis_index(axis)
    bits = []
    size = n // 2
    while size >= 1:
        bits.append((size, lax.rem(me // size, 2)))
        size //= 2
    return bits


def parts_of(x, axis, count):
    size = x.shape[axis] // count
    return [lax.slice_in_dim(x, p * size, (p + 1) * size, axis=axis) for p in range(count)]


def stage_orders(count):
    order = list(range(count))
    return [order, order[::-1]] if count > 1 else [order]


def outer_reduce_scatter(keep, got, axis):
    bits = halves(axis)[:-1]
    count = len(bits)
    orders = stage_orders(count)
    shape = (2,) * count + keep.shape[1:]
    keeps = parts_of(keep.reshape(shape), count, len(orders))
    gots = parts_of(got.reshape(shape), count, len(orders))
    done = []
    for order, y, more in zip(orders, keeps, gots):
        left = list(range(count))
        for b in order:
            at = left.index(b)
            flip_size, bit = bits[b]
            send = pick(y, 1 - bit, at) + pick(more, 1 - bit, at).astype(F32)
            stay = pick(y, bit, at) + pick(more, bit, at).astype(F32)
            more = flip(send.astype(BF16), axis, flip_size)
            y = stay
            left.remove(b)
        done.append(y + more.astype(F32))
    return done


def join(own, got, bit, at):
    return jnp.where(bit == 0, jnp.stack([own, got], at), jnp.stack([got, own], at))


def outer_all_gather(pieces, axis):
    bits = halves(axis)[:-1]
    count = len(bits)
    done = []
    for order, y in zip(stage_orders(count), pieces):
        have = []
        for b in order[::-1]:
            have = sorted(have + [b])
            flip_size, bit = bits[b]
            y = join(y, flip(y, axis, flip_size), bit, have.index(b))
        done.append(y)
    y = jnp.concatenate(done, axis=count) if len(done) > 1 else done[0]
    return y.reshape((2**count,) + y.shape[count:])


CONTRACT_LAST = (((1,), (1,)), ((), ()))


def spectral_kernel(ids, s_ref, r_ref, o_ref):
    o_ref[0] = jnp.dot(r_ref[...], s_ref[...], preferred_element_type=F32).astype(o_ref.dtype)


def spectral_blocks(ids, basis, rotated_t, own, dtype):
    rows = basis.shape[0]
    cols = rotated_t.shape[0]
    count = ids.shape[0]
    tile = min(cols, 256)
    return pl.pallas_call(
        spectral_kernel,
        out_shape=jax.ShapeDtypeStruct((count, cols, own), dtype),
        grid_spec=pltpu.PrefetchScalarGridSpec(
            num_scalar_prefetch=1,
            grid=(count, cols // tile),
            in_specs=[
                pl.BlockSpec((rows, own), lambda g, i, ids: (0, ids[g])),
                pl.BlockSpec((tile, rows), lambda g, i, ids: (i, 0)),
            ],
            out_specs=pl.BlockSpec((1, tile, own), lambda g, i, ids: (g, i, 0)),
        ),
        cost_estimate=pl.CostEstimate(
            flops=2 * count * own * rows * cols, bytes_accessed=2 * count * own * rows, transcendentals=0
        ),
    )(ids, basis, rotated_t)


def back_kernel(core, s_ref, mine_ref, got_ref, o_ref):
    count, _, own = mine_ref.shape
    c = core[0]
    o_ref[...] = jnp.zeros_like(o_ref)

    @pl.loop(0, count)
    def _(j):
        at = pl.multiple_of((2 * j + c) * own, own)
        other = pl.multiple_of((2 * j + 1 - c) * own, own)
        o_ref[0] += lax.dot_general(
            s_ref[:, pl.ds(at, own)], mine_ref[j], CONTRACT_LAST, preferred_element_type=F32
        ) + lax.dot_general(
            s_ref[:, pl.ds(other, own)], got_ref[j], CONTRACT_LAST, preferred_element_type=F32
        )


def back_blocks(core, basis, mine, got, blocks):
    rows, depth = basis.shape
    count, cols, own = mine.shape
    sub = rows // blocks
    whole = pl.BlockSpec((count, cols, own), lambda i, core: (0, 0, 0))
    return pl.pallas_call(
        back_kernel,
        out_shape=jax.ShapeDtypeStruct((blocks, sub, cols), F32),
        grid_spec=pltpu.PrefetchScalarGridSpec(
            num_scalar_prefetch=1,
            grid=(blocks,),
            in_specs=[pl.BlockSpec((sub, depth), lambda i, core: (i, 0)), whole, whole],
            out_specs=pl.BlockSpec((1, sub, cols), lambda i, core: (i, 0, 0)),
        ),
        cost_estimate=pl.CostEstimate(
            flops=2 * rows * depth * cols, bytes_accessed=2 * rows * depth, transcendentals=0
        ),
    )(core, basis, mine, got)


def grad_kernel(reps, scale, *refs):
    rows, columns = refs[:reps], refs[reps : 2 * reps]
    eig_ref, basis_ref, alpha_ref, grad_ref, alpha_scr, grad_scr, weighted_scr = refs[2 * reps :]
    tile, blocks, _ = grad_ref.shape
    for q in range(reps):
        block = rows[q][...]
        weighted_scr[q] = (block.astype(F32) * eig_ref[...] / scale).astype(BF16)
        alpha_scr[pl.ds(q, tile, stride=reps), :] = lax.dot_general(
            block, basis_ref[...], CONTRACT_LAST, preferred_element_type=F32
        )
    alpha_ref[...] = alpha_scr[...].astype(BF16).reshape(alpha_ref.shape)

    sub = columns[0].shape[1]
    for a in range(blocks):
        total = None
        for q in range(reps):
            part = lax.dot_general(
                weighted_scr[q], columns[q][a], CONTRACT_LAST, preferred_element_type=F32
            )
            total = part if total is None else total + part
        for w in range(0, sub, 128):
            grad_scr[w // 128, pl.ds(a, tile, stride=blocks), :] = total[:, w : w + 128]
    for w in range(0, sub, 128):
        grad_ref[:, :, w : w + 128] = (
            grad_scr[w // 128].astype(BF16).reshape(tile, blocks, 128)
        )


def grad_and_alpha(rows, columns, time_eig, time_basis):
    reps = len(rows)
    row_count, times = rows[0].shape
    blocks, sub, _ = columns[0].shape
    time_local = time_basis.shape[0]
    tile = 128
    spec = pl.BlockSpec((tile, times), lambda i: (i, 0))
    full = pl.BlockSpec((blocks, sub, times), lambda i: (0, 0, 0))
    return pl.pallas_call(
        lambda *refs: grad_kernel(reps, reps * times, *refs),
        out_shape=(
            jax.ShapeDtypeStruct((row_count, reps, time_local), BF16),
            jax.ShapeDtypeStruct((row_count, blocks, sub), BF16),
        ),
        grid=(row_count // tile,),
        in_specs=[spec] * reps
        + [full] * reps
        + [
            pl.BlockSpec((1, times), lambda i: (0, 0)),
            pl.BlockSpec((time_local, times), lambda i: (0, 0)),
        ],
        out_specs=(
            pl.BlockSpec((tile, reps, time_local), lambda i: (i, 0, 0)),
            pl.BlockSpec((tile, blocks, sub), lambda i: (i, 0, 0)),
        ),
        scratch_shapes=[
            pltpu.VMEM((tile * reps, time_local), F32),
            pltpu.VMEM((sub // 128, tile * blocks, 128), F32),
            pltpu.VMEM((reps, tile, times), BF16),
        ],
    )(*rows, *columns, time_eig[None, :], time_basis)


def per_device(series, space_basis, time_basis, space_eig, time_eig):
    space_count = lax.axis_size("space")
    time_count = lax.axis_size("tm")
    space_idx = lax.axis_index("space")
    time_idx = lax.axis_index("tm")
    row_count, reps, _ = series.shape
    col_block = space_basis.shape[1]
    own_cols = col_block // space_count
    eig_rows = lax.dynamic_slice_in_dim(
        space_eig, time_idx * col_block + space_idx * own_cols, own_cols
    )
    denom = time_eig[:, None] * eig_rows[None, :] + 0.1
    core = lax.rem(space_idx, 2)
    pairs = jnp.arange(space_count // 2, dtype=jnp.int32) * 2
    order_count = len(stage_orders(len(halves("space")) - 1))
    denoms = parts_of(denom, 0, order_count)

    basis_below, basis_above = line_gather(time_basis, "tm")
    rows, columns = [], []
    first = None
    for q in range(reps):
        mine = series[:, q, :]
        if first is not None:
            mine = lax.optimization_barrier((mine, first))[0]
        below, above = line_gather(mine, "tm")
        first = (below[-1], above[-1])
        turn = (((0,), (1,)), ((), ()))
        rotated = lax.dot_general(time_basis, mine, turn, preferred_element_type=F32)
        for k in range(time_count - 1):
            rotated = rotated + lax.dot_general(
                jnp.concatenate([basis_below[k], basis_above[k]], 0),
                jnp.concatenate([below[k], above[k]], 1),
                turn,
                preferred_element_type=F32,
            )
        rotated = rotated.astype(BF16)
        send = spectral_blocks(pairs + 1 - core, space_basis, rotated, own_cols, BF16)
        got = flip(send, "space", 1)
        keep = spectral_blocks(pairs + core, space_basis, rotated, own_cols, F32)
        spectral = outer_reduce_scatter(keep, got, "space")
        scaled = [(y / d).astype(BF16) for y, d in zip(spectral, denoms)]
        scaled = outer_all_gather(scaled, "space")
        scaled_got = flip(scaled, "space", 1)
        back_part = back_blocks(core[None], space_basis, scaled, scaled_got, time_count)
        back_sub = line_reduce_scatter(back_part, "tm").astype(BF16)
        outer = outer_all_gather(parts_of(back_sub, 0, order_count), "space")
        outer_got = flip(outer, "space", 1)
        columns.append(join(outer, outer_got, core, 1).reshape((space_count,) + back_sub.shape))
        rows.append(line_assemble(back_sub, *line_gather(back_sub, "tm"), "tm"))
    return grad_and_alpha(rows, columns, time_eig, time_basis)


def solution(mesh):
    return jax.shard_map(
        per_device,
        mesh=mesh,
        in_specs=(P("space", None, "tm"), P("space", "tm"), P("tm", None), P(), P()),
        out_specs=(P("space", None, "tm"), P("space", None, "tm")),
        check_vma=False,
    )
```

```python
import jax
import jax.numpy as jnp
from jax import lax
from jax.experimental import pallas as pl
from jax.experimental.pallas import tpu as pltpu
from jax.sharding import PartitionSpec as P


F32 = jnp.float32
BF16 = jnp.bfloat16


def flip(x, axis, bit):
    n = lax.axis_size(axis)
    return lax.ppermute(x, axis, [(i, i ^ bit) for i in range(n)])


def pick(x, index, axis):
    return lax.dynamic_index_in_dim(x, index, axis, keepdims=False)


def line_gather(x, axis):
    n = lax.axis_size(axis)
    up, down, from_below, from_above = x, x, [], []
    for k in range(1, n):
        up = lax.ppermute(up, axis, [(i, i + 1) for i in range(k - 1, n - 1)])
        down = lax.ppermute(down, axis, [(i, i - 1) for i in range(1, n - k + 1)])
        from_below.append(up)
        from_above.append(down)
    return from_below, from_above


def line_reduce_scatter(blocks, axis):
    n = lax.axis_size(axis)
    me = lax.axis_index(axis)
    up = down = None
    for t in range(n - 1):
        send_up = pick(blocks, jnp.minimum(me + n - 1 - t, n - 1), 0)
        send_down = pick(blocks, jnp.maximum(me - (n - 1 - t), 0), 0)
        if t > 0:
            send_up = send_up + up.astype(F32)
            send_down = send_down + down.astype(F32)
        up = lax.ppermute(send_up.astype(BF16), axis, [(i, i + 1) for i in range(t + 1)])
        down = lax.ppermute(
            send_down.astype(BF16), axis, [(i, i - 1) for i in range(n - 1 - t, n)]
        )
    return pick(blocks, me, 0) + (up.astype(F32) + down.astype(F32))


def line_assemble(own, from_below, from_above, axis):
    n = lax.axis_size(axis)
    me = lax.axis_index(axis)
    whole = jnp.zeros((n,) + own.shape, own.dtype)
    whole = lax.dynamic_update_index_in_dim(whole, own, me, 0)
    for k in range(1, n):
        piece = jnp.where(me >= k, from_below[k - 1], from_above[n - k - 1])
        whole = lax.dynamic_update_index_in_dim(whole, piece, lax.rem(me - k + n, n), 0)
    return whole.reshape((-1,) + own.shape[1:])


def halves(axis):
    n = lax.axis_size(axis)
    me = lax.axis_index(axis)
    bits = []
    size = n // 2
    while size >= 1:
        bits.append((size, lax.rem(me // size, 2)))
        size //= 2
    return bits


def parts_of(x, axis, count):
    size = x.shape[axis] // count
    return [lax.slice_in_dim(x, p * size, (p + 1) * size, axis=axis) for p in range(count)]


def stage_orders(count):
    order = list(range(count))
    return [order, order[::-1]] if count > 1 else [order]


def outer_reduce_scatter(keep, got, axis):
    bits = halves(axis)[:-1]
    count = len(bits)
    orders = stage_orders(count)
    shape = (2,) * count + keep.shape[1:]
    keeps = parts_of(keep.reshape(shape), count, len(orders))
    gots = parts_of(got.reshape(shape), count, len(orders))
    done = []
    for order, y, more in zip(orders, keeps, gots):
        left = list(range(count))
        for b in order:
            at = left.index(b)
            flip_size, bit = bits[b]
            send = pick(y, 1 - bit, at) + pick(more, 1 - bit, at).astype(F32)
            stay = pick(y, bit, at) + pick(more, bit, at).astype(F32)
            more = flip(send.astype(BF16), axis, flip_size)
            y = stay
            left.remove(b)
        done.append(y + more.astype(F32))
    return done


def join(own, got, bit, at):
    return jnp.where(bit == 0, jnp.stack([own, got], at), jnp.stack([got, own], at))


def outer_all_gather(pieces, axis):
    bits = halves(axis)[:-1]
    count = len(bits)
    done = []
    for order, y in zip(stage_orders(count), pieces):
        have = []
        for b in order[::-1]:
            have = sorted(have + [b])
            flip_size, bit = bits[b]
            y = join(y, flip(y, axis, flip_size), bit, have.index(b))
        done.append(y)
    y = jnp.concatenate(done, axis=count) if len(done) > 1 else done[0]
    return y.reshape((2**count,) + y.shape[count:])


CONTRACT_LAST = (((1,), (1,)), ((), ()))


def spectral_kernel(ids, s_ref, r_ref, o_ref):
    o_ref[0] = jnp.dot(r_ref[...], s_ref[...], preferred_element_type=F32).astype(o_ref.dtype)


def spectral_blocks(ids, basis, rotated_t, own, dtype):
    rows = basis.shape[0]
    cols = rotated_t.shape[0]
    count = ids.shape[0]
    tile = min(cols, 512)
    return pl.pallas_call(
        spectral_kernel,
        out_shape=jax.ShapeDtypeStruct((count, cols, own), dtype),
        grid_spec=pltpu.PrefetchScalarGridSpec(
            num_scalar_prefetch=1,
            grid=(count, cols // tile),
            in_specs=[
                pl.BlockSpec((rows, own), lambda g, i, ids: (0, ids[g])),
                pl.BlockSpec((tile, rows), lambda g, i, ids: (i, 0)),
            ],
            out_specs=pl.BlockSpec((1, tile, own), lambda g, i, ids: (g, i, 0)),
        ),
        cost_estimate=pl.CostEstimate(
            flops=2 * count * own * rows * cols, bytes_accessed=2 * count * own * rows, transcendentals=0
        ),
    )(ids, basis, rotated_t)


def back_kernel(core, s_ref, mine_ref, got_ref, o_ref):
    count, _, own = mine_ref.shape
    c = core[0]
    o_ref[...] = jnp.zeros_like(o_ref)

    @pl.loop(0, count)
    def _(j):
        at = pl.multiple_of((2 * j + c) * own, own)
        other = pl.multiple_of((2 * j + 1 - c) * own, own)
        o_ref[0] += lax.dot_general(
            s_ref[:, pl.ds(at, own)], mine_ref[j], CONTRACT_LAST, preferred_element_type=F32
        ) + lax.dot_general(
            s_ref[:, pl.ds(other, own)], got_ref[j], CONTRACT_LAST, preferred_element_type=F32
        )


def back_blocks(core, basis, mine, got, blocks):
    rows, depth = basis.shape
    count, cols, own = mine.shape
    sub = rows // blocks
    whole = pl.BlockSpec((count, cols, own), lambda i, core: (0, 0, 0))
    return pl.pallas_call(
        back_kernel,
        out_shape=jax.ShapeDtypeStruct((blocks, sub, cols), F32),
        grid_spec=pltpu.PrefetchScalarGridSpec(
            num_scalar_prefetch=1,
            grid=(blocks,),
            in_specs=[pl.BlockSpec((sub, depth), lambda i, core: (i, 0)), whole, whole],
            out_specs=pl.BlockSpec((1, sub, cols), lambda i, core: (i, 0, 0)),
        ),
        cost_estimate=pl.CostEstimate(
            flops=2 * rows * depth * cols, bytes_accessed=2 * rows * depth, transcendentals=0
        ),
    )(core, basis, mine, got)


def grad_kernel(reps, scale, *refs):
    rows, columns = refs[:reps], refs[reps : 2 * reps]
    eig_ref, basis_ref, alpha_ref, grad_ref, alpha_scr, grad_scr, weighted_scr = refs[2 * reps :]
    tile, blocks, _ = grad_ref.shape
    for q in range(reps):
        block = rows[q][...]
        weighted_scr[q] = (block.astype(F32) * eig_ref[...] / scale).astype(BF16)
        alpha_scr[pl.ds(q, tile, stride=reps), :] = lax.dot_general(
            block, basis_ref[...], CONTRACT_LAST, preferred_element_type=F32
        )
    alpha_ref[...] = alpha_scr[...].astype(BF16).reshape(alpha_ref.shape)

    sub = columns[0].shape[1]
    @pl.loop(0, blocks)
    def _(a):
        total = None
        for q in range(reps):
            part = lax.dot_general(
                weighted_scr[q], columns[q][a], CONTRACT_LAST, preferred_element_type=F32
            )
            total = part if total is None else total + part
        for w in range(0, sub, 128):
            grad_scr[w // 128, pl.ds(a, tile, stride=blocks), :] = total[:, w : w + 128]
    for w in range(0, sub, 128):
        grad_ref[:, :, w : w + 128] = (
            grad_scr[w // 128].astype(BF16).reshape(tile, blocks, 128)
        )


def grad_and_alpha(rows, columns, time_eig, time_basis):
    reps = len(rows)
    row_count, times = rows[0].shape
    blocks, sub, _ = columns[0].shape
    time_local = time_basis.shape[0]
    tile = min(row_count, 512)
    spec = pl.BlockSpec((tile, times), lambda i: (i, 0))
    full = pl.BlockSpec((blocks, sub, times), lambda i: (0, 0, 0))
    return pl.pallas_call(
        lambda *refs: grad_kernel(reps, reps * times, *refs),
        out_shape=(
            jax.ShapeDtypeStruct((row_count, reps, time_local), BF16),
            jax.ShapeDtypeStruct((row_count, blocks, sub), BF16),
        ),
        grid=(row_count // tile,),
        in_specs=[spec] * reps
        + [full] * reps
        + [
            pl.BlockSpec((1, times), lambda i: (0, 0)),
            pl.BlockSpec((time_local, times), lambda i: (0, 0)),
        ],
        out_specs=(
            pl.BlockSpec((tile, reps, time_local), lambda i: (i, 0, 0)),
            pl.BlockSpec((tile, blocks, sub), lambda i: (i, 0, 0)),
        ),
        scratch_shapes=[
            pltpu.VMEM((tile * reps, time_local), F32),
            pltpu.VMEM((sub // 128, tile * blocks, 128), F32),
            pltpu.VMEM((reps, tile, times), BF16),
        ],
    )(*rows, *columns, time_eig[None, :], time_basis)


def per_device(series, space_basis, time_basis, space_eig, time_eig):
    space_count = lax.axis_size("space")
    time_count = lax.axis_size("tm")
    space_idx = lax.axis_index("space")
    time_idx = lax.axis_index("tm")
    row_count, reps, _ = series.shape
    col_block = space_basis.shape[1]
    own_cols = col_block // space_count
    eig_rows = lax.dynamic_slice_in_dim(
        space_eig, time_idx * col_block + space_idx * own_cols, own_cols
    )
    denom = time_eig[:, None] * eig_rows[None, :] + 0.1
    core = lax.rem(space_idx, 2)
    pairs = jnp.arange(space_count // 2, dtype=jnp.int32) * 2
    order_count = len(stage_orders(len(halves("space")) - 1))
    denoms = parts_of(denom, 0, order_count)

    basis_below, basis_above = line_gather(time_basis, "tm")
    rows, columns = [], []
    first = turn_after = None
    for q in range(reps):
        mine = series[:, q, :]
        if first is not None:
            mine = lax.optimization_barrier((mine, first))[0]
        below, above = line_gather(mine, "tm")
        first = (below[max(time_count - 3, 0)], above[max(time_count - 3, 0)])
        turn = (((0,), (1,)), ((), ()))
        rotated = lax.dot_general(time_basis, mine, turn, preferred_element_type=F32)
        for k in range(time_count - 1):
            rotated = rotated + lax.dot_general(
                jnp.concatenate([basis_below[k], basis_above[k]], 0),
                jnp.concatenate([below[k], above[k]], 1),
                turn,
                preferred_element_type=F32,
            )
        rotated = rotated.astype(BF16)
        if turn_after is not None:
            rotated = lax.optimization_barrier((rotated, turn_after))[0]
        send = spectral_blocks(pairs + 1 - core, space_basis, rotated, own_cols, BF16)
        got = flip(send, "space", 1)
        keep = spectral_blocks(pairs + core, space_basis, rotated, own_cols, F32)
        spectral = outer_reduce_scatter(keep, got, "space")
        scaled = [(y / d).astype(BF16) for y, d in zip(spectral, denoms)]
        scaled = outer_all_gather(scaled, "space")
        scaled_got = flip(scaled, "space", 1)
        back_part = back_blocks(core[None], space_basis, scaled, scaled_got, time_count)
        turn_after = back_part
        back_sub = line_reduce_scatter(back_part, "tm").astype(BF16)
        outer = outer_all_gather(parts_of(back_sub, 0, order_count), "space")
        outer_got = flip(outer, "space", 1)
        columns.append(join(outer, outer_got, core, 1).reshape((space_count,) + back_sub.shape))
        rows.append(line_assemble(back_sub, *line_gather(back_sub, "tm"), "tm"))
    return grad_and_alpha(rows, columns, time_eig, time_basis)


def solution(mesh):
    return jax.shard_map(
        per_device,
        mesh=mesh,
        in_specs=(P("space", None, "tm"), P("space", "tm"), P("tm", None), P(), P()),
        out_specs=(P("space", None, "tm"), P("space", None, "tm")),
        check_vma=False,
    )
```

```python
import jax
import jax.numpy as jnp
from jax import lax
from jax.experimental import pallas as pl
from jax.experimental.pallas import tpu as pltpu
from jax.sharding import PartitionSpec as P


F32 = jnp.float32
BF16 = jnp.bfloat16


def flip(x, axis, bit):
    n = lax.axis_size(axis)
    return lax.ppermute(x, axis, [(i, i ^ bit) for i in range(n)])


def pick(x, index, axis):
    return lax.dynamic_index_in_dim(x, index, axis, keepdims=False)


def together(*streams):
    results = [None] * len(streams)
    arrived = {i: next(stream) for i, stream in enumerate(streams)}
    while arrived:
        arrived = lax.optimization_barrier(arrived)
        following = {}
        for i, values in arrived.items():
            try:
                following[i] = streams[i].send(values)
            except StopIteration as stop:
                results[i] = stop.value
        arrived = following
    return results


def line_gather(x, axis):
    n = lax.axis_size(axis)
    up, down, from_below, from_above = x, x, [], []
    for k in range(1, n):
        up = lax.ppermute(up, axis, [(i, i + 1) for i in range(k - 1, n - 1)])
        down = lax.ppermute(down, axis, [(i, i - 1) for i in range(1, n - k + 1)])
        up, down = yield (up, down)
        from_below.append(up)
        from_above.append(down)
    return from_below, from_above


def line_reduce_scatter(blocks, axis):
    n = lax.axis_size(axis)
    me = lax.axis_index(axis)
    up = down = None
    for t in range(n - 1):
        send_up = pick(blocks, jnp.minimum(me + n - 1 - t, n - 1), 0)
        send_down = pick(blocks, jnp.maximum(me - (n - 1 - t), 0), 0)
        if t > 0:
            send_up = send_up + up.astype(F32)
            send_down = send_down + down.astype(F32)
        up = lax.ppermute(send_up.astype(BF16), axis, [(i, i + 1) for i in range(t + 1)])
        down = lax.ppermute(
            send_down.astype(BF16), axis, [(i, i - 1) for i in range(n - 1 - t, n)]
        )
        up, down = yield (up, down)
    return pick(blocks, me, 0) + (up.astype(F32) + down.astype(F32))


def line_assemble(own, from_below, from_above, axis):
    n = lax.axis_size(axis)
    me = lax.axis_index(axis)
    whole = jnp.zeros((n,) + own.shape, own.dtype)
    whole = lax.dynamic_update_index_in_dim(whole, own, me, 0)
    for k in range(1, n):
        piece = jnp.where(me >= k, from_below[k - 1], from_above[n - k - 1])
        whole = lax.dynamic_update_index_in_dim(whole, piece, lax.rem(me - k + n, n), 0)
    return whole.reshape((-1,) + own.shape[1:])


def halves(axis):
    n = lax.axis_size(axis)
    me = lax.axis_index(axis)
    bits = []
    size = n // 2
    while size >= 1:
        bits.append((size, lax.rem(me // size, 2)))
        size //= 2
    return bits


def parts_of(x, axis, count):
    size = x.shape[axis] // count
    return [lax.slice_in_dim(x, p * size, (p + 1) * size, axis=axis) for p in range(count)]


def stage_orders(count):
    order = list(range(count))
    return [order, order[::-1]] if count > 1 else [order]


def outer_reduce_scatter(keep, got, axis):
    bits = halves(axis)[:-1]
    count = len(bits)
    orders = stage_orders(count)
    shape = (2,) * count + keep.shape[1:]
    keeps = parts_of(keep.reshape(shape), count, len(orders))
    gots = parts_of(got.reshape(shape), count, len(orders))
    lefts = [list(range(count)) for _ in orders]
    for stage in range(count):
        arrivals = []
        for p, order in enumerate(orders):
            b = order[stage]
            at = lefts[p].index(b)
            flip_size, bit = bits[b]
            send = pick(keeps[p], 1 - bit, at) + pick(gots[p], 1 - bit, at).astype(F32)
            keeps[p] = pick(keeps[p], bit, at) + pick(gots[p], bit, at).astype(F32)
            arrivals.append(flip(send.astype(BF16), axis, flip_size))
            lefts[p].remove(b)
        gots = yield arrivals
        gots = list(gots)
    return [y + more.astype(F32) for y, more in zip(keeps, gots)]


def join(own, got, bit, at):
    return jnp.where(bit == 0, jnp.stack([own, got], at), jnp.stack([got, own], at))


def space_all_gather(pieces, axis):
    bits = halves(axis)
    count = len(bits) - 1
    orders = stage_orders(count)
    have = [[] for _ in orders]
    pieces = list(pieces)
    for stage in range(count):
        arrivals = []
        for p, order in enumerate(orders):
            b = order[count - 1 - stage]
            have[p] = sorted(have[p] + [b])
            arrivals.append(flip(pieces[p], axis, bits[b][0]))
        arrivals = yield arrivals
        for p, order in enumerate(orders):
            b = order[count - 1 - stage]
            pieces[p] = join(pieces[p], arrivals[p], bits[b][1], have[p].index(b))
    y = jnp.concatenate(pieces, axis=count) if len(pieces) > 1 else pieces[0]
    y = y.reshape((2**count,) + y.shape[count:])
    got = yield flip(y, axis, bits[-1][0])
    return y, got


def spectral_stage(send, keep_of, denoms):
    got = yield flip(send, "space", 1)
    spectral = yield from outer_reduce_scatter(keep_of(), got, "space")
    scaled = [(y / d).astype(BF16) for y, d in zip(spectral, denoms)]
    return (yield from space_all_gather(scaled, "space"))


def back_stage(back_part):
    back_sub = yield from line_reduce_scatter(back_part, "tm")
    back_sub = back_sub.astype(BF16)
    below, above = yield from line_gather(back_sub, "tm")
    return back_sub, below, above


CONTRACT_LAST = (((1,), (1,)), ((), ()))


def spectral_kernel(ids, s_ref, r_ref, o_ref):
    o_ref[0] = jnp.dot(r_ref[...], s_ref[...], preferred_element_type=F32).astype(o_ref.dtype)


def spectral_blocks(ids, basis, rotated_t, own, dtype):
    rows = basis.shape[0]
    cols = rotated_t.shape[0]
    count = ids.shape[0]
    tile = min(cols, 512)
    return pl.pallas_call(
        spectral_kernel,
        out_shape=jax.ShapeDtypeStruct((count, cols, own), dtype),
        grid_spec=pltpu.PrefetchScalarGridSpec(
            num_scalar_prefetch=1,
            grid=(count, cols // tile),
            in_specs=[
                pl.BlockSpec((rows, own), lambda g, i, ids: (0, ids[g])),
                pl.BlockSpec((tile, rows), lambda g, i, ids: (i, 0)),
            ],
            out_specs=pl.BlockSpec((1, tile, own), lambda g, i, ids: (g, i, 0)),
        ),
        cost_estimate=pl.CostEstimate(
            flops=2 * count * own * rows * cols, bytes_accessed=2 * count * own * rows, transcendentals=0
        ),
    )(ids, basis, rotated_t)


def back_kernel(core, s_ref, mine_ref, got_ref, o_ref):
    count, _, own = mine_ref.shape
    c = core[0]
    o_ref[...] = jnp.zeros_like(o_ref)

    @pl.loop(0, count)
    def _(j):
        at = pl.multiple_of((2 * j + c) * own, own)
        other = pl.multiple_of((2 * j + 1 - c) * own, own)
        o_ref[0] += lax.dot_general(
            s_ref[:, pl.ds(at, own)], mine_ref[j], CONTRACT_LAST, preferred_element_type=F32
        ) + lax.dot_general(
            s_ref[:, pl.ds(other, own)], got_ref[j], CONTRACT_LAST, preferred_element_type=F32
        )


def back_blocks(core, basis, mine, got, blocks):
    rows, depth = basis.shape
    count, cols, own = mine.shape
    sub = rows // blocks
    whole = pl.BlockSpec((count, cols, own), lambda i, core: (0, 0, 0))
    return pl.pallas_call(
        back_kernel,
        out_shape=jax.ShapeDtypeStruct((blocks, sub, cols), F32),
        grid_spec=pltpu.PrefetchScalarGridSpec(
            num_scalar_prefetch=1,
            grid=(blocks,),
            in_specs=[pl.BlockSpec((sub, depth), lambda i, core: (i, 0)), whole, whole],
            out_specs=pl.BlockSpec((1, sub, cols), lambda i, core: (i, 0, 0)),
        ),
        cost_estimate=pl.CostEstimate(
            flops=2 * rows * depth * cols, bytes_accessed=2 * rows * depth, transcendentals=0
        ),
    )(core, basis, mine, got)


def grad_kernel(reps, scale, *refs):
    rows, columns = refs[:reps], refs[reps : 2 * reps]
    eig_ref, basis_ref, alpha_ref, grad_ref, alpha_scr, grad_scr, weighted_scr = refs[2 * reps :]
    tile, blocks, _ = grad_ref.shape
    for q in range(reps):
        block = rows[q][...]
        weighted_scr[q] = (block.astype(F32) * eig_ref[...] / scale).astype(BF16)
        alpha_scr[pl.ds(q, tile, stride=reps), :] = lax.dot_general(
            block, basis_ref[...], CONTRACT_LAST, preferred_element_type=F32
        )
    alpha_ref[...] = alpha_scr[...].astype(BF16).reshape(alpha_ref.shape)

    sub = columns[0].shape[1]
    @pl.loop(0, blocks)
    def _(a):
        total = None
        for q in range(reps):
            part = lax.dot_general(
                weighted_scr[q], columns[q][a], CONTRACT_LAST, preferred_element_type=F32
            )
            total = part if total is None else total + part
        for w in range(0, sub, 128):
            grad_scr[w // 128, pl.ds(a, tile, stride=blocks), :] = total[:, w : w + 128]
    for w in range(0, sub, 128):
        grad_ref[:, :, w : w + 128] = (
            grad_scr[w // 128].astype(BF16).reshape(tile, blocks, 128)
        )


def grad_and_alpha(rows, columns, time_eig, time_basis):
    reps = len(rows)
    row_count, times = rows[0].shape
    blocks, sub, _ = columns[0].shape
    time_local = time_basis.shape[0]
    tile = min(row_count, 512)
    spec = pl.BlockSpec((tile, times), lambda i: (i, 0))
    full = pl.BlockSpec((blocks, sub, times), lambda i: (0, 0, 0))
    return pl.pallas_call(
        lambda *refs: grad_kernel(reps, reps * times, *refs),
        out_shape=(
            jax.ShapeDtypeStruct((row_count, reps, time_local), BF16),
            jax.ShapeDtypeStruct((row_count, blocks, sub), BF16),
        ),
        grid=(row_count // tile,),
        in_specs=[spec] * reps
        + [full] * reps
        + [
            pl.BlockSpec((1, times), lambda i: (0, 0)),
            pl.BlockSpec((time_local, times), lambda i: (0, 0)),
        ],
        out_specs=(
            pl.BlockSpec((tile, reps, time_local), lambda i: (i, 0, 0)),
            pl.BlockSpec((tile, blocks, sub), lambda i: (i, 0, 0)),
        ),
        scratch_shapes=[
            pltpu.VMEM((tile * reps, time_local), F32),
            pltpu.VMEM((sub // 128, tile * blocks, 128), F32),
            pltpu.VMEM((reps, tile, times), BF16),
        ],
    )(*rows, *columns, time_eig[None, :], time_basis)


def per_device(series, space_basis, time_basis, space_eig, time_eig):
    space_count = lax.axis_size("space")
    time_count = lax.axis_size("tm")
    space_idx = lax.axis_index("space")
    time_idx = lax.axis_index("tm")
    row_count, reps, _ = series.shape
    col_block = space_basis.shape[1]
    own_cols = col_block // space_count
    eig_rows = lax.dynamic_slice_in_dim(
        space_eig, time_idx * col_block + space_idx * own_cols, own_cols
    )
    denom = time_eig[:, None] * eig_rows[None, :] + 0.1
    core = lax.rem(space_idx, 2)
    pairs = jnp.arange(space_count // 2, dtype=jnp.int32) * 2
    order_count = len(stage_orders(len(halves("space")) - 1))
    denoms = parts_of(denom, 0, order_count)

    turn = (((0,), (1,)), ((), ()))
    mine = [series[:, q, :] for q in range(reps)]
    (basis_below, basis_above), gathered = together(
        line_gather(time_basis, "tm"), line_gather(mine[0], "tm")
    )

    def spectral_of(q, gathered, after):
        below, above = gathered
        rotated = lax.dot_general(time_basis, mine[q], turn, preferred_element_type=F32)
        for k in range(time_count - 1):
            rotated = rotated + lax.dot_general(
                jnp.concatenate([basis_below[k], basis_above[k]], 0),
                jnp.concatenate([below[k], above[k]], 1),
                turn,
                preferred_element_type=F32,
            )
        rotated = rotated.astype(BF16)
        if after is not None:
            rotated = lax.optimization_barrier((rotated, after))[0]
        send = spectral_blocks(pairs + 1 - core, space_basis, rotated, own_cols, BF16)
        return spectral_stage(
            send,
            lambda: spectral_blocks(pairs + core, space_basis, rotated, own_cols, F32),
            denoms,
        )

    def sub_columns(back_sub):
        return space_all_gather(parts_of(back_sub, 0, order_count), "space")

    backs, columns = [], []
    part = None
    for q in range(reps):
        streams = [spectral_of(q, gathered, part)]
        if q + 1 < reps:
            later = lax.optimization_barrier((mine[q + 1], gathered[0][-1]))[0]
            streams.append(line_gather(later, "tm"))
        if part is not None:
            streams.append(back_stage(part))
        done = together(*streams)
        scaled, scaled_got = done[0]
        if q + 1 < reps:
            gathered = done[1]
        if part is not None:
            backs.append(done[-1])
        part = back_blocks(core[None], space_basis, scaled, scaled_got, time_count)
    streams = [line_reduce_scatter(part, "tm")] + [sub_columns(back[0]) for back in backs]
    done = together(*streams)
    columns += done[1:]
    last = done[0].astype(BF16)
    (below, above), last_columns = together(line_gather(last, "tm"), sub_columns(last))
    backs.append((last, below, above))
    columns.append(last_columns)
    rows = [line_assemble(*back, "tm") for back in backs]
    columns = [
        join(own, got, core, 1).reshape((space_count,) + last.shape) for own, got in columns
    ]
    return grad_and_alpha(rows, columns, time_eig, time_basis)


def solution(mesh):
    return jax.shard_map(
        per_device,
        mesh=mesh,
        in_specs=(P("space", None, "tm"), P("space", "tm"), P("tm", None), P(), P()),
        out_specs=(P("space", None, "tm"), P("space", None, "tm")),
        check_vma=False,
    )
```

```python
import jax
import jax.numpy as jnp
from jax import lax
from jax.experimental import pallas as pl
from jax.experimental.pallas import tpu as pltpu
from jax.sharding import PartitionSpec as P


F32 = jnp.float32
BF16 = jnp.bfloat16


def flip(x, axis, bit):
    n = lax.axis_size(axis)
    return lax.ppermute(x, axis, [(i, i ^ bit) for i in range(n)])


def pick(x, index, axis):
    return lax.dynamic_index_in_dim(x, index, axis, keepdims=False)


def together(*streams):
    results = [None] * len(streams)
    arrived = {i: next(stream) for i, stream in enumerate(streams)}
    while arrived:
        arrived = lax.optimization_barrier(arrived)
        following = {}
        for i, values in arrived.items():
            try:
                following[i] = streams[i].send(values)
            except StopIteration as stop:
                results[i] = stop.value
        arrived = following
    return results


def line_gather(x, axis):
    n = lax.axis_size(axis)
    up, down, from_below, from_above = x, x, [], []
    for k in range(1, n):
        up = lax.ppermute(up, axis, [(i, i + 1) for i in range(k - 1, n - 1)])
        down = lax.ppermute(down, axis, [(i, i - 1) for i in range(1, n - k + 1)])
        up, down = yield (up, down)
        from_below.append(up)
        from_above.append(down)
    return from_below, from_above


def line_reduce_scatter(blocks, axis):
    n = lax.axis_size(axis)
    me = lax.axis_index(axis)
    up = down = None
    for t in range(n - 1):
        send_up = pick(blocks, jnp.minimum(me + n - 1 - t, n - 1), 0)
        send_down = pick(blocks, jnp.maximum(me - (n - 1 - t), 0), 0)
        if t > 0:
            send_up = send_up + up.astype(F32)
            send_down = send_down + down.astype(F32)
        up = lax.ppermute(send_up.astype(BF16), axis, [(i, i + 1) for i in range(t + 1)])
        down = lax.ppermute(
            send_down.astype(BF16), axis, [(i, i - 1) for i in range(n - 1 - t, n)]
        )
        up, down = yield (up, down)
    return pick(blocks, me, 0) + (up.astype(F32) + down.astype(F32))


def line_assemble(own, from_below, from_above, axis):
    n = lax.axis_size(axis)
    me = lax.axis_index(axis)
    whole = jnp.zeros((n,) + own.shape, own.dtype)
    whole = lax.dynamic_update_index_in_dim(whole, own, me, 0)
    for k in range(1, n):
        piece = jnp.where(me >= k, from_below[k - 1], from_above[n - k - 1])
        whole = lax.dynamic_update_index_in_dim(whole, piece, lax.rem(me - k + n, n), 0)
    return whole.reshape((-1,) + own.shape[1:])


def halves(axis):
    n = lax.axis_size(axis)
    me = lax.axis_index(axis)
    bits = []
    size = n // 2
    while size >= 1:
        bits.append((size, lax.rem(me // size, 2)))
        size //= 2
    return bits


def parts_of(x, axis, count):
    size = x.shape[axis] // count
    return [lax.slice_in_dim(x, p * size, (p + 1) * size, axis=axis) for p in range(count)]


def stage_orders(count):
    order = list(range(count))
    return [order, order[::-1]] if count > 1 else [order]


def outer_reduce_scatter(keep, got, axis):
    bits = halves(axis)[:-1]
    count = len(bits)
    orders = stage_orders(count)
    shape = (2,) * count + keep.shape[1:]
    keeps = parts_of(keep.reshape(shape), count, len(orders))
    gots = parts_of(got.reshape(shape), count, len(orders))
    lefts = [list(range(count)) for _ in orders]
    for stage in range(count):
        arrivals = []
        for p, order in enumerate(orders):
            b = order[stage]
            at = lefts[p].index(b)
            flip_size, bit = bits[b]
            send = pick(keeps[p], 1 - bit, at) + pick(gots[p], 1 - bit, at).astype(F32)
            keeps[p] = pick(keeps[p], bit, at) + pick(gots[p], bit, at).astype(F32)
            arrivals.append(flip(send.astype(BF16), axis, flip_size))
            lefts[p].remove(b)
        gots = yield arrivals
        gots = list(gots)
    return [y + more.astype(F32) for y, more in zip(keeps, gots)]


def join(own, got, bit, at):
    return jnp.where(bit == 0, jnp.stack([own, got], at), jnp.stack([got, own], at))


def space_all_gather(pieces, axis):
    bits = halves(axis)
    count = len(bits) - 1
    orders = stage_orders(count)
    have = [[] for _ in orders]
    pieces = list(pieces)
    for stage in range(count):
        arrivals = []
        for p, order in enumerate(orders):
            b = order[count - 1 - stage]
            have[p] = sorted(have[p] + [b])
            arrivals.append(flip(pieces[p], axis, bits[b][0]))
        arrivals = yield arrivals
        for p, order in enumerate(orders):
            b = order[count - 1 - stage]
            pieces[p] = join(pieces[p], arrivals[p], bits[b][1], have[p].index(b))
    y = jnp.concatenate(pieces, axis=count) if len(pieces) > 1 else pieces[0]
    y = y.reshape((2**count,) + y.shape[count:])
    got = yield flip(y, axis, bits[-1][0])
    return y, got


def spectral_stage(send, keep_of, denoms):
    got = yield flip(send, "space", 1)
    spectral = yield from outer_reduce_scatter(keep_of(), got, "space")
    scaled = [(y / d).astype(BF16) for y, d in zip(spectral, denoms)]
    return (yield from space_all_gather(scaled, "space"))


def back_stage(back_part):
    back_sub = yield from line_reduce_scatter(back_part, "tm")
    back_sub = back_sub.astype(BF16)
    below, above = yield from line_gather(back_sub, "tm")
    return back_sub, below, above


CONTRACT_LAST = (((1,), (1,)), ((), ()))


def spectral_kernel(ids, s_ref, r_ref, o_ref):
    o_ref[0] = jnp.dot(r_ref[...], s_ref[...], preferred_element_type=F32).astype(o_ref.dtype)


def spectral_blocks(ids, basis, rotated_t, own, dtype):
    rows = basis.shape[0]
    cols = rotated_t.shape[0]
    count = ids.shape[0]
    tile = min(cols, 512)
    return pl.pallas_call(
        spectral_kernel,
        out_shape=jax.ShapeDtypeStruct((count, cols, own), dtype),
        grid_spec=pltpu.PrefetchScalarGridSpec(
            num_scalar_prefetch=1,
            grid=(count, cols // tile),
            in_specs=[
                pl.BlockSpec((rows, own), lambda g, i, ids: (0, ids[g])),
                pl.BlockSpec((tile, rows), lambda g, i, ids: (i, 0)),
            ],
            out_specs=pl.BlockSpec((1, tile, own), lambda g, i, ids: (g, i, 0)),
        ),
        cost_estimate=pl.CostEstimate(
            flops=2 * count * own * rows * cols, bytes_accessed=2 * count * own * rows, transcendentals=0
        ),
    )(ids, basis, rotated_t)


def back_kernel(core, s_ref, mine_ref, got_ref, o_ref):
    count, _, own = mine_ref.shape
    c = core[0]
    o_ref[...] = jnp.zeros_like(o_ref)

    @pl.loop(0, count)
    def _(j):
        at = pl.multiple_of((2 * j + c) * own, own)
        other = pl.multiple_of((2 * j + 1 - c) * own, own)
        o_ref[0] += lax.dot_general(
            s_ref[:, pl.ds(at, own)], mine_ref[j], CONTRACT_LAST, preferred_element_type=F32
        ) + lax.dot_general(
            s_ref[:, pl.ds(other, own)], got_ref[j], CONTRACT_LAST, preferred_element_type=F32
        )


def back_blocks(core, basis, mine, got, blocks):
    rows, depth = basis.shape
    count, cols, own = mine.shape
    sub = rows // blocks
    whole = pl.BlockSpec((count, cols, own), lambda i, core: (0, 0, 0))
    return pl.pallas_call(
        back_kernel,
        out_shape=jax.ShapeDtypeStruct((blocks, sub, cols), F32),
        grid_spec=pltpu.PrefetchScalarGridSpec(
            num_scalar_prefetch=1,
            grid=(blocks,),
            in_specs=[pl.BlockSpec((sub, depth), lambda i, core: (i, 0)), whole, whole],
            out_specs=pl.BlockSpec((1, sub, cols), lambda i, core: (i, 0, 0)),
        ),
        cost_estimate=pl.CostEstimate(
            flops=2 * rows * depth * cols, bytes_accessed=2 * rows * depth, transcendentals=0
        ),
    )(core, basis, mine, got)


def grad_kernel(reps, scale, *refs):
    rows, columns = refs[:reps], refs[reps : 2 * reps]
    eig_ref, basis_ref, alpha_ref, grad_ref, alpha_scr, grad_scr, weighted_scr = refs[2 * reps :]
    tile, blocks, _ = grad_ref.shape
    for q in range(reps):
        block = rows[q][...]
        weighted_scr[q] = (block.astype(F32) * eig_ref[...] / scale).astype(BF16)
        alpha_scr[pl.ds(q, tile, stride=reps), :] = lax.dot_general(
            block, basis_ref[...], CONTRACT_LAST, preferred_element_type=F32
        )
    alpha_ref[...] = alpha_scr[...].astype(BF16).reshape(alpha_ref.shape)

    sub = columns[0].shape[1]
    @pl.loop(0, blocks)
    def _(a):
        total = None
        for q in range(reps):
            part = lax.dot_general(
                weighted_scr[q], columns[q][a], CONTRACT_LAST, preferred_element_type=F32
            )
            total = part if total is None else total + part
        for w in range(0, sub, 128):
            grad_scr[w // 128, pl.ds(a, tile, stride=blocks), :] = total[:, w : w + 128]
    for w in range(0, sub, 128):
        grad_ref[:, :, w : w + 128] = (
            grad_scr[w // 128].astype(BF16).reshape(tile, blocks, 128)
        )


def grad_and_alpha(rows, columns, time_eig, time_basis):
    reps = len(rows)
    row_count, times = rows[0].shape
    blocks, sub, _ = columns[0].shape
    time_local = time_basis.shape[0]
    tile = min(row_count, 512)
    spec = pl.BlockSpec((tile, times), lambda i: (i, 0))
    full = pl.BlockSpec((blocks, sub, times), lambda i: (0, 0, 0))
    return pl.pallas_call(
        lambda *refs: grad_kernel(reps, reps * times, *refs),
        out_shape=(
            jax.ShapeDtypeStruct((row_count, reps, time_local), BF16),
            jax.ShapeDtypeStruct((row_count, blocks, sub), BF16),
        ),
        grid=(row_count // tile,),
        in_specs=[spec] * reps
        + [full] * reps
        + [
            pl.BlockSpec((1, times), lambda i: (0, 0)),
            pl.BlockSpec((time_local, times), lambda i: (0, 0)),
        ],
        out_specs=(
            pl.BlockSpec((tile, reps, time_local), lambda i: (i, 0, 0)),
            pl.BlockSpec((tile, blocks, sub), lambda i: (i, 0, 0)),
        ),
        scratch_shapes=[
            pltpu.VMEM((tile * reps, time_local), F32),
            pltpu.VMEM((sub // 128, tile * blocks, 128), F32),
            pltpu.VMEM((reps, tile, times), BF16),
        ],
    )(*rows, *columns, time_eig[None, :], time_basis)


def per_device(series, space_basis, time_basis, space_eig, time_eig):
    space_count = lax.axis_size("space")
    time_count = lax.axis_size("tm")
    space_idx = lax.axis_index("space")
    time_idx = lax.axis_index("tm")
    row_count, reps, _ = series.shape
    col_block = space_basis.shape[1]
    own_cols = col_block // space_count
    eig_rows = lax.dynamic_slice_in_dim(
        space_eig, time_idx * col_block + space_idx * own_cols, own_cols
    )
    denom = time_eig[:, None] * eig_rows[None, :] + 0.1
    core = lax.rem(space_idx, 2)
    pairs = jnp.arange(space_count // 2, dtype=jnp.int32) * 2
    order_count = len(stage_orders(len(halves("space")) - 1))
    denoms = parts_of(denom, 0, order_count)

    basis_t = time_basis.T
    mine = [series[:, q, :] for q in range(reps)]
    (joined,) = together(line_gather(jnp.concatenate([mine[0], basis_t], 0), "tm"))
    gathered = [[piece[:row_count] for piece in side] for side in joined]
    basis_below, basis_above = [[piece[row_count:] for piece in side] for side in joined]

    def spectral_of(q, gathered, after):
        below, above = gathered
        rotated = lax.dot_general(basis_t, mine[q], CONTRACT_LAST, preferred_element_type=F32)
        for k in range(time_count - 1):
            rotated = rotated + lax.dot_general(
                jnp.concatenate([basis_below[k], basis_above[k]], 1),
                jnp.concatenate([below[k], above[k]], 1),
                CONTRACT_LAST,
                preferred_element_type=F32,
            )
        rotated = rotated.astype(BF16)
        if after is not None:
            rotated = lax.optimization_barrier((rotated, after))[0]
        send = spectral_blocks(pairs + 1 - core, space_basis, rotated, own_cols, BF16)
        return spectral_stage(
            send,
            lambda: spectral_blocks(pairs + core, space_basis, rotated, own_cols, F32),
            denoms,
        )

    def sub_columns(back_sub):
        return space_all_gather(parts_of(back_sub, 0, order_count), "space")

    backs, columns = [], []
    part = None
    for q in range(reps):
        streams = [spectral_of(q, gathered, part)]
        if q + 1 < reps:
            later = lax.optimization_barrier((mine[q + 1], gathered[0][-1]))[0]
            streams.append(line_gather(later, "tm"))
        if part is not None:
            streams.append(back_stage(part))
        done = together(*streams)
        scaled, scaled_got = done[0]
        if q + 1 < reps:
            gathered = done[1]
        if part is not None:
            backs.append(done[-1])
        part = back_blocks(core[None], space_basis, scaled, scaled_got, time_count)
    streams = [line_reduce_scatter(part, "tm")] + [sub_columns(back[0]) for back in backs]
    done = together(*streams)
    columns += done[1:]
    last = done[0].astype(BF16)
    (below, above), last_columns = together(line_gather(last, "tm"), sub_columns(last))
    backs.append((last, below, above))
    columns.append(last_columns)
    rows = [line_assemble(*back, "tm") for back in backs]
    columns = [
        join(own, got, core, 1).reshape((space_count,) + last.shape) for own, got in columns
    ]
    return grad_and_alpha(rows, columns, time_eig, time_basis)


def solution(mesh):
    return jax.shard_map(
        per_device,
        mesh=mesh,
        in_specs=(P("space", None, "tm"), P("space", "tm"), P("tm", None), P(), P()),
        out_specs=(P("space", None, "tm"), P("space", None, "tm")),
        check_vma=False,
    )
```
